256 devices in a mesh: grp: 4 (over z_hi, core), pen: 64 (over z_lo, x, y).
Axes of the slice: x: 4, y: 4, z: 8 (z_hi: 2, z_lo: 4; z = z_hi * 4 + z_lo), core: 2. Of those that a mesh axis runs over, the one named last changes fastest.
Arguments:
- u_field: float32 [2, 2048, 2048], P(None, ('grp', 'pen')), may hold values from -6 to 6
- v_field: float32 [2, 2048, 2048], P(None, ('grp', 'pen')), may hold values from -6 to 6
- ky_order: int32 [2048], replicated, may hold values from 0 to 2047, as said below
Outputs:
- deriv: float32 [2048, 2, 2, 2048], P('grp', None, None, 'pen')
The draws below stay inside these ranges and needn't reach their ends.
Inputs may be any that keep to these rules, and one draw needn't show every extreme that they name: ky_order is a permutation of 0 to 2047; for every position j, ky_order[2047 - j] = (2048 - ky_order[j]) mod 2048, except for the one pair of positions that holds 0 and 1024.
All inputs are finite; a program needn't handle non-finite values.
Results may differ from the reference program's by a relative error of at most 0.00007.
Values sent between devices are 32-bit elements; how exact they have to be, the bound alone decides.
A program may use at most 64 MiB of HBM per device.

```python
import jax
import jax.numpy as jnp
from jax import lax

PLANES = 2
NY = 2048
NZ = 2048


def draw_ky_order(key, part):
    half_length = NY // 2
    order_key = jax.random.fold_in(key, 11)
    side_key = jax.random.fold_in(key, 23)
    pair_index = jax.random.permutation(order_key, half_length).astype(jnp.int32)
    side_flags = jax.random.randint(side_key, (half_length,), 0, 2)
    upper_value = jnp.where(pair_index > 0, NY - pair_index, half_length).astype(jnp.int32)
    first_half = jnp.where(side_flags > 0, upper_value, pair_index)
    second_half = jnp.where(side_flags > 0, pair_index, upper_value)
    return jnp.concatenate([first_half, second_half[::-1]]).astype(jnp.int32)


def shard_levels(key, extent, split, least, high):
    level = 1.0
    for axis_at, parts in split:
        draws = jax.random.uniform(jax.random.fold_in(jax.random.fold_in(key, 6), axis_at), (parts,), jnp.float32, least / len(split), high / len(split))
        level = level * jnp.repeat(jnp.exp(draws), extent[axis_at] // parts).reshape((-1,) + (1,) * (len(extent) - 1 - axis_at))
    return level


def gaussian(key, dims, deviation, bound, shards=(), kind=jnp.bfloat16):
    factor_of = shard_levels(key, dims, shards, -0.22, 0.18) if shards else 1.0
    entries = jax.random.normal(key, dims, jnp.float32) * deviation * factor_of
    return jnp.minimum(jnp.maximum(entries, -bound), bound).astype(kind)


def setup_inputs(seed: int = 0) -> dict:
    key_of = jax.random.split(jax.random.key(seed), 4)
    return {
        "u_field": gaussian(key_of[0], (PLANES, NZ, NY), 1.0, 6.0, ((1, 256),), jnp.float32),
        "v_field": gaussian(key_of[1], (PLANES, NZ, NY), 1.0, 6.0, ((1, 256),), jnp.float32),
        "ky_order": draw_ky_order(jax.random.fold_in(key_of[3], 71), 0),
    }


def signed_scale(length):
    waves = jnp.arange(length)
    signed = jnp.where(waves < length // 2, waves, waves - length)
    signed = jnp.where(waves == length // 2, 0, signed)
    return (2.0 / length) * signed.astype(jnp.float32)


def reference(u_field, v_field, ky_order):
    scale_y = signed_scale(NY)[None, :]
    scale_z = signed_scale(NZ)[:, None]

    def one_plane(pair):
        u_plane, v_plane = pair
        packed = u_plane + 1j * v_plane
        spectrum = jnp.fft.fft2(packed, axes=(0, 1), norm="ortho")
        mirror = jnp.conj(jnp.roll(jnp.flip(spectrum, (0, 1)), (1, 1), (0, 1)))
        first = 0.5 * (spectrum + mirror)
        second = -0.5j * (spectrum - mirror)
        combined = 1j * scale_y * first - scale_z * second
        field = jnp.fft.ifft(combined, axis=0, norm="ortho")
        field = jnp.take(field, ky_order, axis=1)
        return jnp.stack([jnp.real(field), jnp.imag(field)]).astype(jnp.float32)

    planes = lax.map(one_plane, (u_field, v_field))
    return jnp.transpose(planes, (2, 1, 0, 3))
```

```python
import functools
import math

import jax
import jax.numpy as jnp
import numpy as np
from jax import lax
from jax.experimental import pallas as pl
from jax.experimental.pallas import tpu as pltpu
from jax.sharding import PartitionSpec as P

MESH = pl.DeviceIdType.MESH
BLOCK = 128
WAVES = 256
PER_SLAB = 32

def fit(values, degree):
    nodes = 0.125 + 0.125 * np.cos(np.pi * (np.arange(64) + 0.5) / 64)
    series = np.polynomial.Polynomial.fit(nodes, values(np.sqrt(nodes)), degree, domain=[0, 0.25])
    return [float(c) for c in series.convert().coef]


SIN_TERMS = fit(lambda t: np.sin(np.pi * t) / t, 5)
COS_TERMS = fit(lambda t: np.cos(np.pi * t), 5)


def horner(terms, square):
    total = terms[-1]
    for term in terms[-2::-1]:
        total = total * square + term
    return total


def turn(cycles):
    t = cycles - jnp.floor(cycles + 0.5)
    square = t * t
    sine = t * horner(SIN_TERMS, square)
    cosine = horner(COS_TERMS, square)
    return 1.0 - 2.0 * sine * sine, 2.0 * sine * cosine


def split(values):
    high = values.astype(jnp.bfloat16)
    return high, (values - high.astype(jnp.float32)).astype(jnp.bfloat16)


def kernel(
    sizes,
    u_ref,
    v_ref,
    ky_ref,
    filter_hbm,
    out_ref,
    rows_ref,
    sent,
    near,
    far,
    near_side,
    far_side,
    side_out,
    side_in,
    filters,
    sem,
):
    length_y, pens, depth = sizes
    grp, pen = lax.axis_index("grp"), lax.axis_index("pen")
    core = grp % 2
    other = (grp + 2) % 4
    sibling = grp + 1 - 2 * core
    slabs = WAVES // PER_SLAB
    blocks = length_y // BLOCK
    chunks = length_y // WAVES

    barrier = pltpu.get_barrier_semaphore()

    def greet(step, carry):
        target = (pen + step) % pens
        pl.semaphore_signal(barrier, 1, device_id=(other, target), device_id_type=MESH)

        @pl.when(step > 0)
        def _():
            pl.semaphore_signal(barrier, 1, device_id=(grp, target), device_id_type=MESH)

        return carry

    lax.fori_loop(0, pens, greet, 0)
    pl.semaphore_signal(barrier, 1, device_id=(sibling, pen), device_id_type=MESH)

    load = pltpu.make_async_copy(filter_hbm, filters, sem.at[0])
    load.start()

    for b in range(blocks):
        cells = slice(b * BLOCK, (b + 1) * BLOCK)
        piece = jnp.concatenate(
            [u_ref[0, :, cells], u_ref[1, :, cells], v_ref[0, :, cells], v_ref[1, :, cells]], 0
        )
        high, low = split(piece)
        rows_ref[b * 32 : (b + 1) * 32, :] = jnp.concatenate([high, low, high], 1)

    norm = 1.0 / math.sqrt(length_y)
    lane = lax.broadcasted_iota(jnp.int32, (8, 128), 1) // PER_SLAB

    def transform(step):
        chunk = (pen // slabs + step) % chunks
        first = pl.multiple_of(chunk * WAVES, WAVES)
        waves = ky_ref[:, pl.ds(first, WAVES)].astype(jnp.float32)
        cell = lax.broadcasted_iota(jnp.int32, (BLOCK, WAVES), 0).astype(jnp.float32)
        cosine, sine = turn(cell * waves * (1.0 / length_y))
        high, low = split(jnp.concatenate([cosine, sine], 1))
        table = jnp.concatenate([high, high, low], 0)
        product = jnp.dot(rows_ref[...], table, preferred_element_type=jnp.float32)
        start = lax.broadcasted_iota(jnp.int32, (blocks, WAVES), 0).astype(jnp.float32)
        outer_cos, outer_sin = turn(start * waves * (BLOCK / length_y))
        real = jnp.zeros((32, WAVES), jnp.float32)
        imag = jnp.zeros((32, WAVES), jnp.float32)
        for b in range(blocks):
            part_cos = product[b * 32 : (b + 1) * 32, :WAVES]
            part_sin = product[b * 32 : (b + 1) * 32, WAVES:]
            c, s = outer_cos[b : b + 1], outer_sin[b : b + 1]
            real = real + (part_cos * c - part_sin * s)
            imag = imag + (part_cos * s + part_sin * c)
        signed = jnp.where(waves < length_y // 2, waves, waves - length_y)
        signed = jnp.where(waves == length_y // 2, 0.0, signed)
        scale = norm * 2.0 / length_y * signed
        pieces = (
            (-norm * imag[16:24], -norm * imag[24:32], -norm * real[16:24], -norm * real[24:32]),
            (scale * imag[0:8], scale * imag[8:16], scale * real[0:8], scale * real[8:16]),
        )
        for slab in range(slabs):
            half = slice(slab // 4 * 128, slab // 4 * 128 + 128)
            for field in range(2):
                merged = None
                for at in range(4):
                    value = pieces[field][at][:, half]
                    shift = (at - slab) % 4 * PER_SLAB
                    if shift:
                        value = pltpu.roll(value, shift, 1)
                    merged = value if merged is None else jnp.where(lane == at, value, merged)
                sent[chunk * slabs + slab, field * 8 : field * 8 + 8, :] = merged
        return chunk

    def near_copy(target):
        return pltpu.make_async_remote_copy(
            src_ref=sent.at[target],
            dst_ref=near.at[pen],
            send_sem=sem.at[1],
            recv_sem=sem.at[2],
            device_id=(grp, target),
            device_id_type=MESH,
        )

    def far_copy(target):
        return pltpu.make_async_remote_copy(
            src_ref=sent.at[target, pl.ds(0, 8)],
            dst_ref=far.at[pen],
            send_sem=sem.at[3],
            recv_sem=sem.at[4],
            device_id=(other, target),
            device_id_type=MESH,
        )

    def chunk_step(step, carry):
        chunk = transform(step)

        @pl.when(step == 0)
        def _():
            pl.semaphore_wait(barrier, 2 * pens)

        def send(at, inner):
            target = chunk * slabs + (pen + at) % slabs
            far_copy(target).start()

            @pl.when(target != pen)
            def _():
                near_copy(target).start()

            return inner

        return lax.fori_loop(0, slabs, send, carry)

    lax.fori_loop(0, chunks, chunk_step, 0)
    keep = pltpu.make_async_copy(sent.at[pen], near.at[pen], sem.at[5])
    keep.start()

    load.wait()
    keep.wait()
    ahead, behind = 1 + 2 * core, 3 - 2 * core

    def filtered(block, data, kept):
        high, low = split(data)
        taps = filters[block]
        size = data.shape[0]
        wide = jnp.dot(
            taps[:, :size],
            jnp.concatenate([high, low], 1),
            preferred_element_type=jnp.float32,
        )
        narrow = jnp.dot(taps[:, size:], high, preferred_element_type=jnp.float32)
        total = wide[:, :128] + wide[:, 128:] + narrow
        return total if kept is None else total + kept

    pltpu.make_async_copy(near.at[pl.ds(0, pens - 1)], near.at[pl.ds(0, pens - 1)], sem.at[2]).wait()
    own_data = near[:, 0:8, :].reshape(depth, 128)
    side_out[...] = filtered(ahead, own_data, None)
    near_side[...] = filtered(0, own_data, near[:, 8:16, :].reshape(depth, 128))
    pltpu.make_async_copy(far, far, sem.at[4]).wait()
    far_data = far[...].reshape(depth, 128)
    side_out[...] = filtered(behind, far_data, side_out[...])
    across = pltpu.make_async_remote_copy(
        src_ref=side_out,
        dst_ref=side_in,
        send_sem=sem.at[6],
        recv_sem=sem.at[7],
        device_id=(sibling, pen),
        device_id_type=MESH,
    )
    across.start()
    far_side[...] = filtered(2, far_data, near_side[...])
    across.wait()
    out_ref[...] = (far_side[...] + side_in[...]).T
    pltpu.make_async_copy(sent.at[pl.ds(0, pens - 1)], sent.at[pl.ds(0, pens - 1)], sem.at[1]).wait()
    pltpu.make_async_copy(far, far, sem.at[3]).wait()


def filter_table(length, groups):
    waves = np.arange(length)
    scale = np.where(waves < length // 2, waves, waves - length).astype(np.float64)
    scale[length // 2] = 0.0
    taps = np.fft.ifft(2.0 / length * scale).imag
    depth = length // groups
    cell = np.arange(depth)
    table = np.stack([taps[(depth * d + cell[:, None] - cell[None, :]) % length] for d in range(groups)])
    table = table.astype(np.float32)
    high = table.astype(jnp.bfloat16)
    low = (table - high.astype(np.float32)).astype(jnp.bfloat16)
    return np.concatenate([high, low], 2)


def on_device(u_field, v_field, ky_order):
    planes, entry_rows, length_y = u_field.shape
    pens = lax.axis_size("pen")
    groups = lax.axis_size("grp")
    depth = entry_rows * pens
    table = jnp.asarray(filter_table(depth * groups, groups))
    vmem = pl.BlockSpec(memory_space=pltpu.VMEM)
    result = pl.pallas_call(
        functools.partial(kernel, (length_y, pens, depth)),
        out_shape=jax.ShapeDtypeStruct((128, depth), jnp.float32),
        in_specs=[vmem, vmem, vmem, pl.BlockSpec(memory_space=pl.ANY)],
        out_specs=vmem,
        scratch_shapes=[
            pltpu.VMEM((length_y // BLOCK * 32, 3 * BLOCK), jnp.bfloat16),
            pltpu.VMEM((pens, 16, 128), jnp.float32),
            pltpu.VMEM((pens, 16, 128), jnp.float32),
            pltpu.VMEM((pens, 8, 128), jnp.float32),
            pltpu.VMEM((depth, 128), jnp.float32),
            pltpu.VMEM((depth, 128), jnp.float32),
            pltpu.VMEM((depth, 128), jnp.float32),
            pltpu.VMEM((depth, 128), jnp.float32),
            pltpu.VMEM((groups, depth, 2 * depth), jnp.bfloat16),
            pltpu.SemaphoreType.DMA((8,)),
        ],
        compiler_params=pltpu.CompilerParams(
            collective_id=0, has_side_effects=True, vmem_limit_bytes=48 * 1024 * 1024
        ),
    )(u_field, v_field, ky_order.reshape(1, length_y), table)
    result = result.reshape(2, planes, length_y // pens, depth)
    return jnp.transpose(result, (3, 0, 1, 2))


def solution(mesh):
    placed = (P(None, ("grp", "pen"), None), P(None, ("grp", "pen"), None), P())
    return jax.shard_map(
        on_device,
        mesh=mesh,
        in_specs=placed,
        out_specs=P("grp", None, None, "pen"),
        check_vma=False,
    )
```

```python
import functools
import math

import jax
import jax.numpy as jnp
import numpy as np
from jax import lax
from jax.experimental import pallas as pl
from jax.experimental.pallas import tpu as pltpu
from jax.sharding import PartitionSpec as P

MESH = pl.DeviceIdType.MESH
BLOCK = 128
WAVES = 256
PER_SLAB = 32

def fit(values, degree):
    nodes = 0.125 + 0.125 * np.cos(np.pi * (np.arange(64) + 0.5) / 64)
    series = np.polynomial.Polynomial.fit(nodes, values(np.sqrt(nodes)), degree, domain=[0, 0.25])
    return [float(c) for c in series.convert().coef]


SIN_TERMS = fit(lambda t: np.sin(np.pi * t) / t, 5)
COS_TERMS = fit(lambda t: np.cos(np.pi * t), 5)


def horner(terms, square):
    total = terms[-1]
    for term in terms[-2::-1]:
        total = total * square + term
    return total


def turn(cycles):
    t = cycles - jnp.floor(cycles + 0.5)
    square = t * t
    sine = t * horner(SIN_TERMS, square)
    cosine = horner(COS_TERMS, square)
    return 1.0 - 2.0 * sine * sine, 2.0 * sine * cosine


def split(values):
    high = values.astype(jnp.bfloat16)
    return high, (values - high.astype(jnp.float32)).astype(jnp.bfloat16)


def kernel(
    sizes,
    u_hbm,
    v_hbm,
    ky_hbm,
    filter_hbm,
    out_ref,
    u_ref,
    v_ref,
    ky_ref,
    rows_ref,
    sent,
    near,
    far,
    near_side,
    far_side,
    side_out,
    side_in,
    filters,
    sem,
    ready,
):
    length_y, pens, depth = sizes
    grp, pen = lax.axis_index("grp"), lax.axis_index("pen")
    core = grp % 2
    other = (grp + 2) % 4
    sibling = grp + 1 - 2 * core
    half = grp // 2
    slabs = WAVES // PER_SLAB
    blocks = length_y // BLOCK
    chunks = length_y // 2 // WAVES
    mirrored = pen >= pens // 2
    own_slab = jnp.where(mirrored, pens - 1 - pen, pen)

    inputs = [
        pltpu.make_async_copy(ky_hbm, ky_ref, sem.at[8]),
        pltpu.make_async_copy(u_hbm, u_ref, sem.at[9]),
        pltpu.make_async_copy(v_hbm, v_ref, sem.at[10]),
    ]
    for copy in inputs:
        copy.start()
    barrier = pltpu.get_barrier_semaphore()

    signal = functools.partial(pl.semaphore_signal, inc=1, device_id_type=MESH)
    signal(barrier, device_id=(sibling, pen))

    def greet(step, carry):
        signal(barrier, device_id=(grp, (pen + step) % pens))
        return carry

    lax.fori_loop(1, pens, greet, 0)

    @pl.when(half == 0)
    def _():
        def greet_far(step, carry):
            signal(barrier, device_id=(other, (pen + step) % pens))
            return carry

        lax.fori_loop(0, pens, greet_far, 0)

    load = pltpu.make_async_copy(filter_hbm, filters, sem.at[0])
    load.start()
    for copy in inputs:
        copy.wait()

    for b in range(blocks):
        cells = slice(b * BLOCK, (b + 1) * BLOCK)
        piece = jnp.concatenate(
            [u_ref[0, :, cells], u_ref[1, :, cells], v_ref[0, :, cells], v_ref[1, :, cells]], 0
        )
        high, low = split(piece)
        rows_ref[b * 32 : (b + 1) * 32, :] = jnp.concatenate([high, low, high], 1)

    norm = 1.0 / math.sqrt(length_y)
    lane = lax.broadcasted_iota(jnp.int32, (8, 128), 1) // PER_SLAB

    def nth_chunk(step):
        return (own_slab // slabs + step) % chunks

    def transform(step):
        chunk = nth_chunk(step)
        first = pl.multiple_of(chunk * WAVES, WAVES)
        waves = ky_ref[:, pl.ds(first, WAVES)].astype(jnp.float32)
        cell = lax.broadcasted_iota(jnp.int32, (BLOCK, WAVES), 0).astype(jnp.float32)
        cosine, sine = turn(cell * waves * (1.0 / length_y))
        parity = 1.0 - 2.0 * (lax.broadcasted_iota(jnp.int32, (BLOCK, WAVES), 0) % 2).astype(jnp.float32)
        sine = jnp.where(waves == 0, parity, jnp.where(waves == length_y // 2, 1.0, sine))
        high, low = split(jnp.concatenate([cosine, sine], 1))
        table = jnp.concatenate([high, high, low], 0)
        product = jnp.dot(rows_ref[...], table, preferred_element_type=jnp.float32)
        start = lax.broadcasted_iota(jnp.int32, (blocks, WAVES), 0).astype(jnp.float32)
        outer_cos, outer_sin = turn(start * waves * (BLOCK / length_y))
        real = jnp.zeros((32, WAVES), jnp.float32)
        imag = jnp.zeros((32, WAVES), jnp.float32)
        for b in range(blocks):
            part_cos = product[b * 32 : (b + 1) * 32, :WAVES]
            part_sin = product[b * 32 : (b + 1) * 32, WAVES:]
            c, s = outer_cos[b : b + 1], outer_sin[b : b + 1]
            real = real + (part_cos * c - part_sin * s)
            imag = imag + (part_cos * s + part_sin * c)
        signed = jnp.where(waves < length_y // 2, waves, waves - length_y)
        signed = jnp.where(waves == length_y // 2, 0.0, signed)
        scale = norm * 2.0 / length_y * signed
        pieces = (
            (-norm * imag[16:24], -norm * imag[24:32], -norm * real[16:24], -norm * real[24:32]),
            (scale * imag[0:8], scale * imag[8:16], scale * real[0:8], scale * real[8:16]),
        )
        for slab in range(slabs):
            half = slice(slab // 4 * 128, slab // 4 * 128 + 128)
            for field in range(2):
                merged = None
                for at in range(4):
                    value = pieces[field][at][:, half]
                    shift = (at - slab) % 4 * PER_SLAB
                    if shift:
                        value = pltpu.roll(value, shift, 1)
                    merged = value if merged is None else jnp.where(lane == at, value, merged)
                sent[chunk * slabs + slab, field * 8 : field * 8 + 8, :] = merged
        return None

    def near_copy(field, slab, target):
        part = pl.ds(field * 8, 8)
        return pltpu.make_async_remote_copy(
            src_ref=sent.at[slab, part],
            dst_ref=near.at[pen, part],
            send_sem=sem.at[1],
            recv_sem=sem.at[2 + 9 * field],
            device_id=(grp, target),
            device_id_type=MESH,
        )

    def far_copy(slab, target):
        return pltpu.make_async_remote_copy(
            src_ref=sent.at[slab, pl.ds(0, 8)],
            dst_ref=far.at[pen],
            send_sem=sem.at[3],
            recv_sem=sem.at[4],
            device_id=(other, target),
            device_id_type=MESH,
        )

    def nth(at):
        place = (pen + at) % (2 * slabs)
        slab = nth_chunk(at // (2 * slabs)) * slabs + place % slabs
        return slab, jnp.where(place < slabs, slab, pens - 1 - slab)

    def send_near(field, low, high):
        def body(at, carry):
            slab, target = nth(at)

            @pl.when(target != pen)
            def _():
                near_copy(field, slab, target).start()

            return carry

        lax.fori_loop(low * 2 * slabs, high * 2 * slabs, body, 0)

    def send_far(low, high):
        def body(at, carry):
            far_copy(*nth(at)).start()
            return carry

        lax.fori_loop(low * 2 * slabs, high * 2 * slabs, body, 0)

    across = pen // 4 % 4 + pen % 4
    hold = jnp.where(half == 0, (pen // 16 + across) // 2, across * 3 // 4)
    hold = jnp.maximum(chunks - 1 - hold, 0)

    def chunk_step(step, carry):
        transform(step)

        @pl.when(step == hold)
        def _():
            pl.semaphore_wait(barrier, jnp.where(half == 0, pens, 2 * pens))

        low = jnp.where(step == hold, 0, step)

        @pl.when((half == 1) & (step == hold))
        def _():
            def answer(at, inner):
                signal(ready, device_id=(other, (pen + at) % pens))
                return inner

            lax.fori_loop(0, pens, answer, 0)

        @pl.when((half == 1) & (step >= hold))
        def _():
            send_far(low, step + 1)

        @pl.when(step >= hold)
        def _():
            send_near(0, low, step + 1)

        return carry

    lax.fori_loop(0, chunks, chunk_step, 0)
    keep = pltpu.make_async_copy(sent.at[own_slab], near.at[pen], sem.at[5])
    keep.start()
    send_near(1, 0, chunks)

    @pl.when(half == 0)
    def _():
        pl.semaphore_wait(ready, pens)
        send_far(0, chunks)

    block = ky_ref[:, pl.ds(pl.multiple_of(own_slab // 4 * 128, 128), 128)]
    lane1 = lax.broadcasted_iota(jnp.int32, (1, 128), 1)
    waves = jnp.zeros((1, 128), jnp.int32)
    for at in range(4):
        shifted = pltpu.roll(block, (at - own_slab % 4 + 4) % 4 * PER_SLAB, 1)
        waves = jnp.where(lane1 // PER_SLAB == at, shifted, waves)
    alone = jnp.broadcast_to((waves == 0) | (waves == length_y // 2), (128, 128))
    row = lax.broadcasted_iota(jnp.int32, (128, 128), 0)
    column = lax.broadcasted_iota(jnp.int32, (128, 128), 1)
    plain = jnp.where((row == column) & ~(alone & (row < 64)), 1.0, 0.0)
    reverse = row // PER_SLAB * PER_SLAB + PER_SLAB - 1 - row % PER_SLAB
    turned = jnp.where((reverse == column) & ~alone, jnp.where(row < 64, 1.0, -1.0), 0.0)
    turned = jnp.where((reverse - 64 == column) & alone, -1.0, turned)
    pick = jnp.where(mirrored, turned, plain).astype(jnp.bfloat16)
    pick = jnp.concatenate([pick, pick, pick], 1)
    flip = jnp.where(mirrored, -1.0, 1.0)

    load.wait()
    keep.wait()
    ahead, behind = 1 + 2 * core, 3 - 2 * core

    def filtered(block, data, kept):
        high, low = split(data)
        taps = filters[block]
        size = data.shape[0]
        wide = jnp.dot(
            taps[:, :size],
            jnp.concatenate([high, low], 1),
            preferred_element_type=jnp.float32,
        )
        narrow = jnp.dot(taps[:, size:], high, preferred_element_type=jnp.float32)
        total = wide[:, :128] + wide[:, 128:] + narrow
        return total if kept is None else total + kept

    def received(at):
        count = near.at[pl.ds(0, pens - 1), pl.ds(0, 8)]
        pltpu.make_async_copy(count, count, sem.at[at]).wait()

    received(2)
    own_data = near[:, 0:8, :].reshape(depth, 128)
    side_out[...] = filtered(ahead, own_data, None)
    near_side[...] = filtered(0, own_data, None)
    pltpu.make_async_copy(far, far, sem.at[4]).wait()
    far_data = far[...].reshape(depth, 128)
    side_out[...] = filtered(behind, far_data, side_out[...])
    swap = pltpu.make_async_remote_copy(
        src_ref=side_out,
        dst_ref=side_in,
        send_sem=sem.at[6],
        recv_sem=sem.at[7],
        device_id=(sibling, pen),
        device_id_type=MESH,
    )
    swap.start()
    far_side[...] = filtered(2, far_data, near_side[...])
    received(11)
    swap.wait()
    total = near[:, 8:16, :].reshape(depth, 128) + flip * (far_side[...] + side_in[...])
    high, low = split(total)
    lowest = (total - high.astype(jnp.float32) - low.astype(jnp.float32)).astype(jnp.bfloat16)
    out_ref[...] = lax.dot_general(
        pick,
        jnp.concatenate([high, low, lowest], 1),
        (((1,), (1,)), ((), ())),
        preferred_element_type=jnp.float32,
    )
    both = near.at[pl.ds(0, pens - 1)]
    pltpu.make_async_copy(both, both, sem.at[1]).wait()
    pltpu.make_async_copy(far, far, sem.at[3]).wait()


def filter_table(length, groups):
    waves = np.arange(length)
    scale = np.where(waves < length // 2, waves, waves - length).astype(np.float64)
    scale[length // 2] = 0.0
    taps = np.fft.ifft(2.0 / length * scale).imag
    depth = length // groups
    cell = np.arange(depth)
    table = np.stack([taps[(depth * d + cell[:, None] - cell[None, :]) % length] for d in range(groups)])
    table = table.astype(np.float32)
    high = table.astype(jnp.bfloat16)
    low = (table - high.astype(np.float32)).astype(jnp.bfloat16)
    return np.concatenate([high, low], 2)


def on_device(u_field, v_field, ky_order):
    planes, entry_rows, length_y = u_field.shape
    pens = lax.axis_size("pen")
    groups = lax.axis_size("grp")
    depth = entry_rows * pens
    table = jnp.asarray(filter_table(depth * groups, groups))
    inputs = (u_field, v_field, ky_order.reshape(1, length_y), table)
    inputs = [pltpu.with_memory_space_constraint(value, pltpu.HBM) for value in inputs]
    vmem = pl.BlockSpec(memory_space=pltpu.VMEM)
    result = pl.pallas_call(
        functools.partial(kernel, (length_y, pens, depth)),
        out_shape=jax.ShapeDtypeStruct((128, depth), jnp.float32),
        in_specs=[pl.BlockSpec(memory_space=pltpu.HBM)] * 4,
        out_specs=vmem,
        scratch_shapes=[
            pltpu.VMEM(u_field.shape, jnp.float32),
            pltpu.VMEM(v_field.shape, jnp.float32),
            pltpu.VMEM((1, length_y), jnp.int32),
            pltpu.VMEM((length_y // BLOCK * 32, 3 * BLOCK), jnp.bfloat16),
            pltpu.VMEM((pens // 2, 16, 128), jnp.float32),
            pltpu.VMEM((pens, 16, 128), jnp.float32),
            pltpu.VMEM((pens, 8, 128), jnp.float32),
            pltpu.VMEM((depth, 128), jnp.float32),
            pltpu.VMEM((depth, 128), jnp.float32),
            pltpu.VMEM((depth, 128), jnp.float32),
            pltpu.VMEM((depth, 128), jnp.float32),
            pltpu.VMEM((groups, depth, 2 * depth), jnp.bfloat16),
            pltpu.SemaphoreType.DMA((12,)),
            pltpu.SemaphoreType.REGULAR,
        ],
        compiler_params=pltpu.CompilerParams(
            collective_id=0, has_side_effects=True, vmem_limit_bytes=32 * 1024 * 1024
        ),
    )(*inputs)
    result = result.reshape(2, planes, length_y // pens, depth)
    return jnp.transpose(result, (3, 0, 1, 2))


def solution(mesh):
    placed = (P(None, ("grp", "pen"), None), P(None, ("grp", "pen"), None), P())
    return jax.shard_map(
        on_device,
        mesh=mesh,
        in_specs=placed,
        out_specs=P("grp", None, None, "pen"),
        check_vma=False,
    )
```

```python
import functools
import math

import jax
import jax.numpy as jnp
import numpy as np
from jax import lax
from jax.experimental import pallas as pl
from jax.experimental.pallas import tpu as pltpu
from jax.sharding import PartitionSpec as P

MESH = pl.DeviceIdType.MESH
BLOCK = 128
WAVES = 256
PER_SLAB = 32

def fit(values, degree):
    nodes = 0.125 + 0.125 * np.cos(np.pi * (np.arange(64) + 0.5) / 64)
    series = np.polynomial.Polynomial.fit(nodes, values(np.sqrt(nodes)), degree, domain=[0, 0.25])
    return [float(c) for c in series.convert().coef]


SIN_TERMS = fit(lambda t: np.sin(np.pi * t) / t, 5)
COS_TERMS = fit(lambda t: np.cos(np.pi * t), 5)


def horner(terms, square):
    total = terms[-1]
    for term in terms[-2::-1]:
        total = total * square + term
    return total


def turn(cycles):
    t = cycles - jnp.floor(cycles + 0.5)
    square = t * t
    sine = t * horner(SIN_TERMS, square)
    cosine = horner(COS_TERMS, square)
    return 1.0 - 2.0 * sine * sine, 2.0 * sine * cosine


def split(values):
    high = values.astype(jnp.bfloat16)
    return high, (values - high.astype(jnp.float32)).astype(jnp.bfloat16)


def kernel(
    sizes,
    u_hbm,
    v_hbm,
    ky_hbm,
    filter_hbm,
    out_ref,
    u_ref,
    v_ref,
    ky_ref,
    rows_ref,
    sent,
    near,
    far,
    near_side,
    far_side,
    side_out,
    side_in,
    filters,
    sem,
    ready,
):
    length_y, pens, depth = sizes
    grp, pen = lax.axis_index("grp"), lax.axis_index("pen")
    core = grp % 2
    other = (grp + 2) % 4
    sibling = grp + 1 - 2 * core
    half = grp // 2
    slabs = WAVES // PER_SLAB
    blocks = length_y // BLOCK
    chunks = length_y // 2 // WAVES
    mirrored = pen >= pens // 2
    own_slab = jnp.where(mirrored, pens - 1 - pen, pen)
    own_class = own_slab // slabs
    slot = own_class * 2 * slabs + jnp.where(mirrored, slabs, 0) + own_slab % slabs

    inputs = [
        pltpu.make_async_copy(ky_hbm, ky_ref, sem.at[8]),
        pltpu.make_async_copy(u_hbm, u_ref, sem.at[9]),
        pltpu.make_async_copy(v_hbm, v_ref, sem.at[10]),
    ]
    for copy in inputs:
        copy.start()
    barrier = pltpu.get_barrier_semaphore()

    signal = functools.partial(pl.semaphore_signal, inc=1, device_id_type=MESH)
    signal(barrier, device_id=(sibling, pen))

    def greet(step, carry):
        signal(barrier, device_id=(grp, (pen + step) % pens))
        return carry

    lax.fori_loop(1, pens, greet, 0, unroll=7)

    @pl.when(half == 0)
    def _():
        def greet_far(step, carry):
            signal(barrier, device_id=(other, (pen + step) % pens))
            return carry

        lax.fori_loop(0, pens, greet_far, 0, unroll=8)

    load = pltpu.make_async_copy(filter_hbm, filters, sem.at[0])
    load.start()
    for copy in inputs:
        copy.wait()

    for b in range(blocks):
        cells = slice(b * BLOCK, (b + 1) * BLOCK)
        piece = jnp.concatenate(
            [u_ref[0, :, cells], u_ref[1, :, cells], v_ref[0, :, cells], v_ref[1, :, cells]], 0
        )
        high, low = split(piece)
        rows_ref[b * 32 : (b + 1) * 32, :] = jnp.concatenate([high, low, high], 1)

    norm = 1.0 / math.sqrt(length_y)
    lane = lax.broadcasted_iota(jnp.int32, (8, 128), 1) // PER_SLAB

    def nth_chunk(step):
        return (own_slab // slabs + step) % chunks

    def transform(step):
        chunk = nth_chunk(step)
        first = pl.multiple_of(chunk * WAVES, WAVES)
        waves = ky_ref[:, pl.ds(first, WAVES)].astype(jnp.float32)
        cell = lax.broadcasted_iota(jnp.int32, (BLOCK, WAVES), 0).astype(jnp.float32)
        cosine, sine = turn(cell * waves * (1.0 / length_y))
        parity = 1.0 - 2.0 * (lax.broadcasted_iota(jnp.int32, (BLOCK, WAVES), 0) % 2).astype(jnp.float32)
        sine = jnp.where(waves == 0, parity, jnp.where(waves == length_y // 2, 1.0, sine))
        high, low = split(jnp.concatenate([cosine, sine], 1))
        table = jnp.concatenate([high, high, low], 0)
        product = jnp.dot(rows_ref[...], table, preferred_element_type=jnp.float32)
        start = lax.broadcasted_iota(jnp.int32, (blocks, WAVES), 0).astype(jnp.float32)
        outer_cos, outer_sin = turn(start * waves * (BLOCK / length_y))
        real = jnp.zeros((32, WAVES), jnp.float32)
        imag = jnp.zeros((32, WAVES), jnp.float32)
        for b in range(blocks):
            part_cos = product[b * 32 : (b + 1) * 32, :WAVES]
            part_sin = product[b * 32 : (b + 1) * 32, WAVES:]
            c, s = outer_cos[b : b + 1], outer_sin[b : b + 1]
            real = real + (part_cos * c - part_sin * s)
            imag = imag + (part_cos * s + part_sin * c)
        signed = jnp.where(waves < length_y // 2, waves, waves - length_y)
        signed = jnp.where(waves == length_y // 2, 0.0, signed)
        scale = norm * 2.0 / length_y * signed
        pieces = (
            (-norm * imag[16:24], -norm * imag[24:32], -norm * real[16:24], -norm * real[24:32]),
            (scale * imag[0:8], scale * imag[8:16], scale * real[0:8], scale * real[8:16]),
        )
        for slab in range(slabs):
            half = slice(slab // 4 * 128, slab // 4 * 128 + 128)
            for field in range(2):
                merged = None
                for at in range(4):
                    value = pieces[field][at][:, half]
                    shift = (at - slab) % 4 * PER_SLAB
                    if shift:
                        value = pltpu.roll(value, shift, 1)
                    merged = value if merged is None else jnp.where(lane == at, value, merged)
                sent[chunk * slabs + slab, field * 8 : field * 8 + 8, :] = merged
        return None

    def near_copy(field, slab, target):
        part = pl.ds(field * 8, 8)
        return pltpu.make_async_remote_copy(
            src_ref=sent.at[slab, part],
            dst_ref=near.at[pen if field else slot, part],
            send_sem=sem.at[1],
            recv_sem=sem.at[2 + 9 * field],
            device_id=(grp, target),
            device_id_type=MESH,
        )

    def far_copy(slab, target, piece):
        return pltpu.make_async_remote_copy(
            src_ref=sent.at[slab, pl.ds(0, 8)],
            dst_ref=far.at[slot],
            send_sem=sem.at[3],
            recv_sem=sem.at[4 + 8 * piece],
            device_id=(other, target),
            device_id_type=MESH,
        )

    def nth(at):
        place = (pen + at) % (2 * slabs)
        slab = nth_chunk(at // (2 * slabs)) * slabs + place % slabs
        return slab, jnp.where(place < slabs, slab, pens - 1 - slab)

    def send_near(field, low, high):
        def body(at, carry):
            slab, target = nth(at)

            @pl.when(target != pen)
            def _():
                near_copy(field, slab, target).start()

            return carry

        lax.fori_loop(low * 2 * slabs, high * 2 * slabs, body, 0)

    def send_far(low, high):
        def body(at, carry):
            far_copy(*nth(at), at // (4 * slabs)).start()
            return carry

        lax.fori_loop(low * 2 * slabs, high * 2 * slabs, body, 0)

    across = pen // 4 % 4 + pen % 4
    hold = jnp.where(half == 0, (pen // 16 + across) // 2, across * 3 // 4)
    hold = jnp.maximum(chunks - 1 - hold, 0)

    def chunk_step(step, carry):
        transform(step)

        @pl.when(step == hold)
        def _():
            pl.semaphore_wait(barrier, jnp.where(half == 0, pens, 2 * pens))

        low = jnp.where(step == hold, 0, step)

        @pl.when((half == 1) & (step == hold))
        def _():
            signal(ready, device_id=(other, pen))

        @pl.when((half == 1) & (step >= hold))
        def _():
            send_far(low, step + 1)

        @pl.when(step >= hold)
        def _():
            send_near(0, low, step + 1)

        return carry

    lax.fori_loop(0, chunks, chunk_step, 0)
    keep_v = pltpu.make_async_copy(
        sent.at[own_slab, pl.ds(0, 8)], near.at[slot, pl.ds(0, 8)], sem.at[5]
    )
    keep_u = pltpu.make_async_copy(
        sent.at[own_slab, pl.ds(8, 8)], near.at[pen, pl.ds(8, 8)], sem.at[13]
    )
    keep_v.start()
    keep_u.start()

    @pl.when(half == 0)
    def _():
        pl.semaphore_wait(ready, 1)
        send_far(0, chunks)

    send_near(1, 0, chunks)

    block = ky_ref[:, pl.ds(pl.multiple_of(own_slab // 4 * 128, 128), 128)]
    lane1 = lax.broadcasted_iota(jnp.int32, (1, 128), 1)
    waves = jnp.zeros((1, 128), jnp.int32)
    for at in range(4):
        shifted = pltpu.roll(block, (at - own_slab % 4 + 4) % 4 * PER_SLAB, 1)
        waves = jnp.where(lane1 // PER_SLAB == at, shifted, waves)
    alone = jnp.broadcast_to((waves == 0) | (waves == length_y // 2), (128, 128))
    row = lax.broadcasted_iota(jnp.int32, (128, 128), 0)
    column = lax.broadcasted_iota(jnp.int32, (128, 128), 1)
    plain = jnp.where((row == column) & ~(alone & (row < 64)), 1.0, 0.0)
    reverse = row // PER_SLAB * PER_SLAB + PER_SLAB - 1 - row % PER_SLAB
    turned = jnp.where((reverse == column) & ~alone, jnp.where(row < 64, 1.0, -1.0), 0.0)
    turned = jnp.where((reverse - 64 == column) & alone, -1.0, turned)
    pick = jnp.where(mirrored, turned, plain).astype(jnp.bfloat16)
    pick = jnp.concatenate([pick, pick, pick], 1)
    flip = jnp.where(mirrored, -1.0, 1.0)

    load.wait()
    keep_v.wait()
    keep_u.wait()
    ahead, behind = 1 + 2 * core, 3 - 2 * core

    def filtered(block, data, kept):
        high, low = split(data)
        taps = filters[block]
        size = data.shape[0]
        wide = jnp.dot(
            taps[:, :size],
            jnp.concatenate([high, low], 1),
            preferred_element_type=jnp.float32,
        )
        narrow = jnp.dot(taps[:, size:], high, preferred_element_type=jnp.float32)
        total = wide[:, :128] + wide[:, 128:] + narrow
        return total if kept is None else total + kept

    def received(at):
        count = near.at[pl.ds(0, pens - 1), pl.ds(0, 8)]
        pltpu.make_async_copy(count, count, sem.at[at]).wait()

    received(2)
    own_data = near[:, 0:8, :].reshape(depth, 128)
    side_out[...] = filtered(ahead, own_data, None)
    near_side[...] = filtered(0, own_data, None)
    def far_part(block, piece, rows):
        data, high_taps, low_taps = [], [], []
        for at in range(2):
            sender = (own_class + 2 * chunks - 2 * piece - at) % chunks
            cells = 2 * slabs * 8
            first = pl.multiple_of(sender * cells, cells)
            data.append(far[pl.ds(sender * 2 * slabs, 2 * slabs)].reshape(cells, 128))
            high_taps.append(filters[block, rows, pl.ds(first, cells)])
            low_taps.append(filters[block, rows, pl.ds(first + depth, cells)])
        high, low = split(jnp.concatenate(data, 0))
        wide = jnp.dot(
            jnp.concatenate(high_taps, 1),
            jnp.concatenate([high, low], 1),
            preferred_element_type=jnp.float32,
        )
        narrow = jnp.dot(
            jnp.concatenate(low_taps, 1), high, preferred_element_type=jnp.float32
        )
        return wide[:, :128] + wide[:, 128:] + narrow

    def far_received(piece):
        count = far.at[pl.ds(0, pens // 2)]
        pltpu.make_async_copy(count, count, sem.at[4 + 8 * piece]).wait()

    every = pl.ds(0, depth)
    far_received(0)
    side_out[...] += far_part(behind, 0, every)
    near_side[...] += far_part(2, 0, every)
    far_received(1)
    swaps = []
    for at in range(2):
        rows = pl.ds(at * depth // 2, depth // 2)
        side_out[rows, :] += far_part(behind, 1, rows)
        swaps.append(
            pltpu.make_async_remote_copy(
                src_ref=side_out.at[rows],
                dst_ref=side_in.at[rows],
                send_sem=sem.at[6 + 8 * at],
                recv_sem=sem.at[7 + 8 * at],
                device_id=(sibling, pen),
                device_id_type=MESH,
            )
        )
        swaps[at].start()
    far_side[...] = near_side[...] + far_part(2, 1, every)
    received(11)
    for swap in swaps:
        swap.wait()
    total = near[:, 8:16, :].reshape(depth, 128) + flip * (far_side[...] + side_in[...])
    high, low = split(total)
    lowest = (total - high.astype(jnp.float32) - low.astype(jnp.float32)).astype(jnp.bfloat16)
    out_ref[...] = lax.dot_general(
        pick,
        jnp.concatenate([high, low, lowest], 1),
        (((1,), (1,)), ((), ())),
        preferred_element_type=jnp.float32,
    )
    both = near.at[pl.ds(0, pens - 1)]
    pltpu.make_async_copy(both, both, sem.at[1]).wait()
    pltpu.make_async_copy(far, far, sem.at[3]).wait()


def filter_table(length, groups):
    waves = np.arange(length)
    scale = np.where(waves < length // 2, waves, waves - length).astype(np.float64)
    scale[length // 2] = 0.0
    taps = np.fft.ifft(2.0 / length * scale).imag
    depth = length // groups
    cell = np.arange(depth)
    pens = depth // 8
    lower = np.arange(pens // 2).reshape(-1, WAVES // PER_SLAB)
    pen = np.concatenate([lower, pens - 1 - lower], 1).reshape(-1, 1)
    source = (pen * 8 + np.arange(8)).reshape(-1)
    table = np.stack([taps[(depth * d + cell[:, None] - source[None, :]) % length] for d in range(groups)])
    table = table.astype(np.float32)
    high = table.astype(jnp.bfloat16)
    low = (table - high.astype(np.float32)).astype(jnp.bfloat16)
    return np.concatenate([high, low], 2)


def on_device(u_field, v_field, ky_order):
    planes, entry_rows, length_y = u_field.shape
    pens = lax.axis_size("pen")
    groups = lax.axis_size("grp")
    depth = entry_rows * pens
    table = jnp.asarray(filter_table(depth * groups, groups))
    inputs = (u_field, v_field, ky_order.reshape(1, length_y), table)
    inputs = [pltpu.with_memory_space_constraint(value, pltpu.HBM) for value in inputs]
    vmem = pl.BlockSpec(memory_space=pltpu.VMEM)
    result = pl.pallas_call(
        functools.partial(kernel, (length_y, pens, depth)),
        out_shape=jax.ShapeDtypeStruct((128, depth), jnp.float32),
        in_specs=[pl.BlockSpec(memory_space=pltpu.HBM)] * 4,
        out_specs=vmem,
        scratch_shapes=[
            pltpu.VMEM(u_field.shape, jnp.float32),
            pltpu.VMEM(v_field.shape, jnp.float32),
            pltpu.VMEM((1, length_y), jnp.int32),
            pltpu.VMEM((length_y // BLOCK * 32, 3 * BLOCK), jnp.bfloat16),
            pltpu.VMEM((pens // 2, 16, 128), jnp.float32),
            pltpu.VMEM((pens, 16, 128), jnp.float32),
            pltpu.VMEM((pens, 8, 128), jnp.float32),
            pltpu.VMEM((depth, 128), jnp.float32),
            pltpu.VMEM((depth, 128), jnp.float32),
            pltpu.VMEM((depth, 128), jnp.float32),
            pltpu.VMEM((depth, 128), jnp.float32),
            pltpu.VMEM((groups, depth, 2 * depth), jnp.bfloat16),
            pltpu.SemaphoreType.DMA((16,)),
            pltpu.SemaphoreType.REGULAR,
        ],
        compiler_params=pltpu.CompilerParams(
            collective_id=0, has_side_effects=True, vmem_limit_bytes=32 * 1024 * 1024
        ),
    )(*inputs)
    result = result.reshape(2, planes, length_y // pens, depth)
    return jnp.transpose(result, (3, 0, 1, 2))


def solution(mesh):
    placed = (P(None, ("grp", "pen"), None), P(None, ("grp", "pen"), None), P())
    return jax.shard_map(
        on_device,
        mesh=mesh,
        in_specs=placed,
        out_specs=P("grp", None, None, "pen"),
        check_vma=False,
    )
```

```python
import functools
import math

import jax
import jax.numpy as jnp
import numpy as np
from jax import lax
from jax.experimental import pallas as pl
from jax.experimental.pallas import tpu as pltpu
from jax.sharding import PartitionSpec as P

MESH = pl.DeviceIdType.MESH
BLOCK = 128
WAVES = 256
PER_SLAB = 32

def fit(values, degree):
    nodes = 0.125 + 0.125 * np.cos(np.pi * (np.arange(64) + 0.5) / 64)
    series = np.polynomial.Polynomial.fit(nodes, values(np.sqrt(nodes)), degree, domain=[0, 0.25])
    return [float(c) for c in series.convert().coef]


SIN_TERMS = fit(lambda t: np.sin(np.pi * t) / t, 5)
COS_TERMS = fit(lambda t: np.cos(np.pi * t), 5)


def horner(terms, square):
    total = terms[-1]
    for term in terms[-2::-1]:
        total = total * square + term
    return total


def turn(cycles):
    t = cycles - jnp.floor(cycles + 0.5)
    square = t * t
    sine = t * horner(SIN_TERMS, square)
    cosine = horner(COS_TERMS, square)
    return 1.0 - 2.0 * sine * sine, 2.0 * sine * cosine


def split(values):
    high = values.astype(jnp.bfloat16)
    return high, (values - high.astype(jnp.float32)).astype(jnp.bfloat16)


def kernel(
    sizes,
    u_hbm,
    v_hbm,
    ky_hbm,
    filter_hbm,
    out_ref,
    u_ref,
    v_ref,
    ky_ref,
    rows_ref,
    sent,
    near,
    far,
    near_side,
    far_side,
    side_out,
    side_in,
    filters,
    sem,
    ready,
):
    length_y, pens, depth = sizes
    grp, pen = lax.axis_index("grp"), lax.axis_index("pen")
    core = grp % 2
    other = (grp + 2) % 4
    sibling = grp + 1 - 2 * core
    half = grp // 2
    slabs = WAVES // PER_SLAB
    blocks = length_y // BLOCK
    chunks = length_y // 2 // WAVES
    mirrored = pen >= pens // 2
    own_slab = jnp.where(mirrored, pens - 1 - pen, pen)
    own_class = own_slab // slabs
    slot = own_class * 2 * slabs + jnp.where(mirrored, slabs, 0) + own_slab % slabs

    inputs = [
        pltpu.make_async_copy(ky_hbm, ky_ref, sem.at[8]),
        pltpu.make_async_copy(u_hbm, u_ref, sem.at[9]),
        pltpu.make_async_copy(v_hbm, v_ref, sem.at[10]),
    ]
    for copy in inputs:
        copy.start()
    barrier = pltpu.get_barrier_semaphore()

    signal = functools.partial(pl.semaphore_signal, inc=1, device_id_type=MESH)
    signal(barrier, device_id=(sibling, pen))

    def greet(step, carry):
        signal(barrier, device_id=(grp, (pen + step) % pens))
        return carry

    lax.fori_loop(1, pens, greet, 0, unroll=7)

    @pl.when(half == 0)
    def _():
        def greet_far(step, carry):
            signal(barrier, device_id=(other, (pen + step) % pens))
            return carry

        lax.fori_loop(0, pens, greet_far, 0, unroll=8)

    load = pltpu.make_async_copy(filter_hbm, filters, sem.at[0])
    load.start()
    for copy in inputs:
        copy.wait()

    for b in range(blocks):
        cells = slice(b * BLOCK, (b + 1) * BLOCK)
        piece = jnp.concatenate(
            [u_ref[0, :, cells], u_ref[1, :, cells], v_ref[0, :, cells], v_ref[1, :, cells]], 0
        )
        high, low = split(piece)
        rows_ref[b * 32 : (b + 1) * 32, :] = jnp.concatenate([high, low, high], 1)

    norm = 1.0 / math.sqrt(length_y)
    lane = lax.broadcasted_iota(jnp.int32, (8, 128), 1) // PER_SLAB

    def nth_chunk(step):
        return (own_slab // slabs + step) % chunks

    def transform(step):
        chunk = nth_chunk(step)
        first = pl.multiple_of(chunk * WAVES, WAVES)
        waves = ky_ref[:, pl.ds(first, WAVES)].astype(jnp.float32)
        cell = lax.broadcasted_iota(jnp.int32, (BLOCK, WAVES), 0).astype(jnp.float32)
        cosine, sine = turn(cell * waves * (1.0 / length_y))
        parity = 1.0 - 2.0 * (lax.broadcasted_iota(jnp.int32, (BLOCK, WAVES), 0) % 2).astype(jnp.float32)
        sine = jnp.where(waves == 0, parity, jnp.where(waves == length_y // 2, 1.0, sine))
        high, low = split(jnp.concatenate([cosine, sine], 1))
        table = jnp.concatenate([high, high, low], 0)
        product = jnp.dot(rows_ref[...], table, preferred_element_type=jnp.float32)
        start = lax.broadcasted_iota(jnp.int32, (blocks, WAVES), 0).astype(jnp.float32)
        outer_cos, outer_sin = turn(start * waves * (BLOCK / length_y))
        real = jnp.zeros((32, WAVES), jnp.float32)
        imag = jnp.zeros((32, WAVES), jnp.float32)
        for b in range(blocks):
            part_cos = product[b * 32 : (b + 1) * 32, :WAVES]
            part_sin = product[b * 32 : (b + 1) * 32, WAVES:]
            c, s = outer_cos[b : b + 1], outer_sin[b : b + 1]
            real = real + (part_cos * c - part_sin * s)
            imag = imag + (part_cos * s + part_sin * c)
        signed = jnp.where(waves < length_y // 2, waves, waves - length_y)
        signed = jnp.where(waves == length_y // 2, 0.0, signed)
        scale = norm * 2.0 / length_y * signed
        pieces = (
            (-norm * imag[16:24], -norm * imag[24:32], -norm * real[16:24], -norm * real[24:32]),
            (scale * imag[0:8], scale * imag[8:16], scale * real[0:8], scale * real[8:16]),
        )
        for slab in range(slabs):
            half = slice(slab // 4 * 128, slab // 4 * 128 + 128)
            for field in range(2):
                merged = None
                for at in range(4):
                    value = pieces[field][at][:, half]
                    shift = (at - slab) % 4 * PER_SLAB
                    if shift:
                        value = pltpu.roll(value, shift, 1)
                    merged = value if merged is None else jnp.where(lane == at, value, merged)
                sent[chunk * slabs + slab, field * 8 : field * 8 + 8, :] = merged
        return None

    def near_copy(field, slab, target):
        part = pl.ds(field * 8, 8)
        return pltpu.make_async_remote_copy(
            src_ref=sent.at[slab, part],
            dst_ref=near.at[pen if field else slot, part],
            send_sem=sem.at[1],
            recv_sem=sem.at[2 + 9 * field],
            device_id=(grp, target),
            device_id_type=MESH,
        )

    def far_copy(slab, target, piece):
        return pltpu.make_async_remote_copy(
            src_ref=sent.at[slab, pl.ds(0, 8)],
            dst_ref=far.at[slot],
            send_sem=sem.at[3],
            recv_sem=sem.at[4 + 8 * piece],
            device_id=(other, target),
            device_id_type=MESH,
        )

    def nth(at):
        place = (pen + at) % (2 * slabs)
        slab = nth_chunk(at // (2 * slabs)) * slabs + place % slabs
        return slab, jnp.where(place < slabs, slab, pens - 1 - slab)

    def send_near(field, low, high):
        def body(at, carry):
            slab, target = nth(at)

            @pl.when(target != pen)
            def _():
                near_copy(field, slab, target).start()

            return carry

        lax.fori_loop(low * 2 * slabs, high * 2 * slabs, body, 0)

    def send_far(low, high):
        def body(at, carry):
            far_copy(*nth(at), at // (4 * slabs)).start()
            return carry

        lax.fori_loop(low * 2 * slabs, high * 2 * slabs, body, 0)

    across = pen // 4 % 4 + pen % 4
    hold = jnp.where(half == 0, (pen // 16 + across) // 2, across * 2 // 3)
    hold = jnp.maximum(chunks - 1 - hold, 0)

    def chunk_step(step, carry):
        transform(step)

        @pl.when(step == hold)
        def _():
            pl.semaphore_wait(barrier, jnp.where(half == 0, pens, 2 * pens))

        low = jnp.where(step == hold, 0, step)

        @pl.when((half == 1) & (step == hold))
        def _():
            signal(ready, device_id=(other, pen))

        @pl.when((half == 1) & (step >= hold))
        def _():
            send_far(low, step + 1)

        @pl.when((half == 0) & (step >= hold))
        def _():
            send_near(0, low, step + 1)

        return carry

    lax.fori_loop(0, chunks, chunk_step, 0)
    keep_v = pltpu.make_async_copy(
        sent.at[own_slab, pl.ds(0, 8)], near.at[slot, pl.ds(0, 8)], sem.at[5]
    )
    keep_u = pltpu.make_async_copy(
        sent.at[own_slab, pl.ds(8, 8)], near.at[pen, pl.ds(8, 8)], sem.at[13]
    )
    keep_v.start()
    keep_u.start()

    @pl.when(half == 0)
    def _():
        pl.semaphore_wait(ready, 1)
        send_far(0, chunks)

    @pl.when(half == 1)
    def _():
        send_near(0, 0, chunks)

    send_near(1, 0, chunks)

    block = ky_ref[:, pl.ds(pl.multiple_of(own_slab // 4 * 128, 128), 128)]
    lane1 = lax.broadcasted_iota(jnp.int32, (1, 128), 1)
    waves = jnp.zeros((1, 128), jnp.int32)
    for at in range(4):
        shifted = pltpu.roll(block, (at - own_slab % 4 + 4) % 4 * PER_SLAB, 1)
        waves = jnp.where(lane1 // PER_SLAB == at, shifted, waves)
    alone = jnp.broadcast_to((waves == 0) | (waves == length_y // 2), (128, 128))
    row = lax.broadcasted_iota(jnp.int32, (128, 128), 0)
    column = lax.broadcasted_iota(jnp.int32, (128, 128), 1)
    plain = jnp.where((row == column) & ~(alone & (row < 64)), 1.0, 0.0)
    reverse = row // PER_SLAB * PER_SLAB + PER_SLAB - 1 - row % PER_SLAB
    turned = jnp.where((reverse == column) & ~alone, jnp.where(row < 64, 1.0, -1.0), 0.0)
    turned = jnp.where((reverse - 64 == column) & alone, -1.0, turned)
    pick = jnp.where(mirrored, turned, plain).astype(jnp.bfloat16)
    pick = jnp.concatenate([pick, pick, pick], 1)
    flip = jnp.where(mirrored, -1.0, 1.0)

    load.wait()
    keep_v.wait()
    keep_u.wait()
    ahead, behind = 1 + 2 * core, 3 - 2 * core

    def filtered(block, data, kept):
        high, low = split(data)
        taps = filters[block]
        size = data.shape[0]
        wide = jnp.dot(
            taps[:, :size],
            jnp.concatenate([high, low], 1),
            preferred_element_type=jnp.float32,
        )
        narrow = jnp.dot(taps[:, size:], high, preferred_element_type=jnp.float32)
        total = wide[:, :128] + wide[:, 128:] + narrow
        return total if kept is None else total + kept

    def received(at):
        count = near.at[pl.ds(0, pens - 1), pl.ds(0, 8)]
        pltpu.make_async_copy(count, count, sem.at[at]).wait()

    received(2)
    own_data = near[:, 0:8, :].reshape(depth, 128)
    side_out[...] = filtered(ahead, own_data, None)
    near_side[...] = filtered(0, own_data, None)
    def far_part(block, piece, rows):
        data, high_taps, low_taps = [], [], []
        for at in range(2):
            sender = (own_class + 2 * chunks - 2 * piece - at) % chunks
            cells = 2 * slabs * 8
            first = pl.multiple_of(sender * cells, cells)
            data.append(far[pl.ds(sender * 2 * slabs, 2 * slabs)].reshape(cells, 128))
            high_taps.append(filters[block, rows, pl.ds(first, cells)])
            low_taps.append(filters[block, rows, pl.ds(first + depth, cells)])
        high, low = split(jnp.concatenate(data, 0))
        wide = jnp.dot(
            jnp.concatenate(high_taps, 1),
            jnp.concatenate([high, low], 1),
            preferred_element_type=jnp.float32,
        )
        narrow = jnp.dot(
            jnp.concatenate(low_taps, 1), high, preferred_element_type=jnp.float32
        )
        return wide[:, :128] + wide[:, 128:] + narrow

    def far_received(piece):
        count = far.at[pl.ds(0, pens // 2)]
        pltpu.make_async_copy(count, count, sem.at[4 + 8 * piece]).wait()

    every = pl.ds(0, depth)
    far_received(0)
    side_out[...] += far_part(behind, 0, every)
    near_side[...] += far_part(2, 0, every)
    far_received(1)
    swaps = []
    for at in range(2):
        rows = pl.ds(at * depth // 2, depth // 2)
        side_out[rows, :] += far_part(behind, 1, rows)
        swaps.append(
            pltpu.make_async_remote_copy(
                src_ref=side_out.at[rows],
                dst_ref=side_in.at[rows],
                send_sem=sem.at[6 + 8 * at],
                recv_sem=sem.at[7 + 8 * at],
                device_id=(sibling, pen),
                device_id_type=MESH,
            )
        )
        swaps[at].start()
    far_side[...] = near_side[...] + far_part(2, 1, every)
    received(11)
    for swap in swaps:
        swap.wait()
    total = near[:, 8:16, :].reshape(depth, 128) + flip * (far_side[...] + side_in[...])
    high, low = split(total)
    lowest = (total - high.astype(jnp.float32) - low.astype(jnp.float32)).astype(jnp.bfloat16)
    out_ref[...] = lax.dot_general(
        pick,
        jnp.concatenate([high, low, lowest], 1),
        (((1,), (1,)), ((), ())),
        preferred_element_type=jnp.float32,
    )
    both = near.at[pl.ds(0, pens - 1)]
    pltpu.make_async_copy(both, both, sem.at[1]).wait()
    pltpu.make_async_copy(far, far, sem.at[3]).wait()


def filter_table(length, groups):
    waves = np.arange(length)
    scale = np.where(waves < length // 2, waves, waves - length).astype(np.float64)
    scale[length // 2] = 0.0
    taps = np.fft.ifft(2.0 / length * scale).imag
    depth = length // groups
    cell = np.arange(depth)
    pens = depth // 8
    lower = np.arange(pens // 2).reshape(-1, WAVES // PER_SLAB)
    pen = np.concatenate([lower, pens - 1 - lower], 1).reshape(-1, 1)
    source = (pen * 8 + np.arange(8)).reshape(-1)
    table = np.stack([taps[(depth * d + cell[:, None] - source[None, :]) % length] for d in range(groups)])
    table = table.astype(np.float32)
    high = table.astype(jnp.bfloat16)
    low = (table - high.astype(np.float32)).astype(jnp.bfloat16)
    return np.concatenate([high, low], 2)


def on_device(u_field, v_field, ky_order):
    planes, entry_rows, length_y = u_field.shape
    pens = lax.axis_size("pen")
    groups = lax.axis_size("grp")
    depth = entry_rows * pens
    table = jnp.asarray(filter_table(depth * groups, groups))
    inputs = (u_field, v_field, ky_order.reshape(1, length_y), table)
    inputs = [pltpu.with_memory_space_constraint(value, pltpu.HBM) for value in inputs]
    vmem = pl.BlockSpec(memory_space=pltpu.VMEM)
    result = pl.pallas_call(
        functools.partial(kernel, (length_y, pens, depth)),
        out_shape=jax.ShapeDtypeStruct((128, depth), jnp.float32),
        in_specs=[pl.BlockSpec(memory_space=pltpu.HBM)] * 4,
        out_specs=vmem,
        scratch_shapes=[
            pltpu.VMEM(u_field.shape, jnp.float32),
            pltpu.VMEM(v_field.shape, jnp.float32),
            pltpu.VMEM((1, length_y), jnp.int32),
            pltpu.VMEM((length_y // BLOCK * 32, 3 * BLOCK), jnp.bfloat16),
            pltpu.VMEM((pens // 2, 16, 128), jnp.float32),
            pltpu.VMEM((pens, 16, 128), jnp.float32),
            pltpu.VMEM((pens, 8, 128), jnp.float32),
            pltpu.VMEM((depth, 128), jnp.float32),
            pltpu.VMEM((depth, 128), jnp.float32),
            pltpu.VMEM((depth, 128), jnp.float32),
            pltpu.VMEM((depth, 128), jnp.float32),
            pltpu.VMEM((groups, depth, 2 * depth), jnp.bfloat16),
            pltpu.SemaphoreType.DMA((16,)),
            pltpu.SemaphoreType.REGULAR,
        ],
        compiler_params=pltpu.CompilerParams(
            collective_id=0, has_side_effects=True, vmem_limit_bytes=32 * 1024 * 1024
        ),
    )(*inputs)
    result = result.reshape(2, planes, length_y // pens, depth)
    return jnp.transpose(result, (3, 0, 1, 2))


def solution(mesh):
    placed = (P(None, ("grp", "pen"), None), P(None, ("grp", "pen"), None), P())
    return jax.shard_map(
        on_device,
        mesh=mesh,
        in_specs=placed,
        out_specs=P("grp", None, None, "pen"),
        check_vma=False,
    )
```

```python
import functools
import math

import jax
import jax.numpy as jnp
import numpy as np
from jax import lax
from jax.experimental import pallas as pl
from jax.experimental.pallas import tpu as pltpu
from jax.sharding import PartitionSpec as P

MESH = pl.DeviceIdType.MESH
BLOCK = 128
WAVES = 256
PER_SLAB = 32

def fit(values, degree):
    nodes = 0.125 + 0.125 * np.cos(np.pi * (np.arange(64) + 0.5) / 64)
    series = np.polynomial.Polynomial.fit(nodes, values(np.sqrt(nodes)), degree, domain=[0, 0.25])
    return [float(c) for c in series.convert().coef]


SIN_TERMS = fit(lambda t: np.sin(np.pi * t) / t, 5)
COS_TERMS = fit(lambda t: np.cos(np.pi * t), 5)


def horner(terms, square):
    total = terms[-1]
    for term in terms[-2::-1]:
        total = total * square + term
    return total


def turn(cycles):
    t = cycles - jnp.floor(cycles + 0.5)
    square = t * t
    sine = t * horner(SIN_TERMS, square)
    cosine = horner(COS_TERMS, square)
    return 1.0 - 2.0 * sine * sine, 2.0 * sine * cosine


def split(values):
    high = values.astype(jnp.bfloat16)
    return high, (values - high.astype(jnp.float32)).astype(jnp.bfloat16)


def kernel(
    sizes,
    u_hbm,
    v_hbm,
    ky_hbm,
    filter_hbm,
    out_ref,
    u_ref,
    v_ref,
    ky_ref,
    rows_ref,
    sent,
    near,
    far,
    near_side,
    far_side,
    side_out,
    side_in,
    filters,
    sem,
    ready,
):
    length_y, pens, depth = sizes
    grp, pen = lax.axis_index("grp"), lax.axis_index("pen")
    core = grp % 2
    other = (grp + 2) % 4
    sibling = grp + 1 - 2 * core
    half = grp // 2
    slabs = WAVES // PER_SLAB
    blocks = length_y // BLOCK
    chunks = length_y // 2 // WAVES
    mirrored = pen >= pens // 2
    own_slab = jnp.where(mirrored, pens - 1 - pen, pen)
    own_class = own_slab // slabs
    slot = own_class * 2 * slabs + jnp.where(mirrored, slabs, 0) + own_slab % slabs

    inputs = [
        pltpu.make_async_copy(ky_hbm, ky_ref, sem.at[8]),
        pltpu.make_async_copy(u_hbm, u_ref, sem.at[9]),
        pltpu.make_async_copy(v_hbm, v_ref, sem.at[10]),
    ]
    for copy in inputs:
        copy.start()
    barrier = pltpu.get_barrier_semaphore()

    signal = functools.partial(pl.semaphore_signal, inc=1, device_id_type=MESH)
    signal(barrier, device_id=(sibling, pen))

    def greet(step, carry):
        signal(barrier, device_id=(grp, (pen + step) % pens))
        return carry

    lax.fori_loop(1, pens, greet, 0, unroll=7)

    @pl.when(half == 0)
    def _():
        def greet_far(step, carry):
            signal(barrier, device_id=(other, (pen + step) % pens))
            return carry

        lax.fori_loop(0, pens, greet_far, 0, unroll=8)

    load = pltpu.make_async_copy(filter_hbm, filters, sem.at[0])
    load.start()
    for copy in inputs:
        copy.wait()

    for b in range(blocks):
        cells = slice(b * BLOCK, (b + 1) * BLOCK)
        piece = jnp.concatenate(
            [u_ref[0, :, cells], u_ref[1, :, cells], v_ref[0, :, cells], v_ref[1, :, cells]], 0
        )
        high, low = split(piece)
        rows_ref[b * 32 : (b + 1) * 32, :] = jnp.concatenate([high, low, high], 1)

    norm = 1.0 / math.sqrt(length_y)
    lane = lax.broadcasted_iota(jnp.int32, (8, 128), 1) // PER_SLAB

    def nth_chunk(step):
        return (own_slab // slabs + step) % chunks

    def transform(step):
        chunk = nth_chunk(step)
        first = pl.multiple_of(chunk * WAVES, WAVES)
        waves = ky_ref[:, pl.ds(first, WAVES)].astype(jnp.float32)
        cell = lax.broadcasted_iota(jnp.int32, (BLOCK, WAVES), 0).astype(jnp.float32)
        cosine, sine = turn(cell * waves * (1.0 / length_y))
        parity = 1.0 - 2.0 * (lax.broadcasted_iota(jnp.int32, (BLOCK, WAVES), 0) % 2).astype(jnp.float32)
        sine = jnp.where(waves == 0, parity, jnp.where(waves == length_y // 2, 1.0, sine))
        high, low = split(jnp.concatenate([cosine, sine], 1))
        table = jnp.concatenate([high, high, low], 0)
        product = jnp.dot(rows_ref[...], table, preferred_element_type=jnp.float32)
        start = lax.broadcasted_iota(jnp.int32, (blocks, WAVES), 0).astype(jnp.float32)
        outer_cos, outer_sin = turn(start * waves * (BLOCK / length_y))
        real = jnp.zeros((32, WAVES), jnp.float32)
        imag = jnp.zeros((32, WAVES), jnp.float32)
        for b in range(blocks):
            part_cos = product[b * 32 : (b + 1) * 32, :WAVES]
            part_sin = product[b * 32 : (b + 1) * 32, WAVES:]
            c, s = outer_cos[b : b + 1], outer_sin[b : b + 1]
            real = real + (part_cos * c - part_sin * s)
            imag = imag + (part_cos * s + part_sin * c)
        signed = jnp.where(waves < length_y // 2, waves, waves - length_y)
        signed = jnp.where(waves == length_y // 2, 0.0, signed)
        scale = norm * 2.0 / length_y * signed
        pieces = (
            (-norm * imag[16:24], -norm * imag[24:32], -norm * real[16:24], -norm * real[24:32]),
            (scale * imag[0:8], scale * imag[8:16], scale * real[0:8], scale * real[8:16]),
        )
        for slab in range(slabs):
            half = slice(slab // 4 * 128, slab // 4 * 128 + 128)
            for field in range(2):
                merged = None
                for at in range(4):
                    value = pieces[field][at][:, half]
                    shift = (at - slab) % 4 * PER_SLAB
                    if shift:
                        value = pltpu.roll(value, shift, 1)
                    merged = value if merged is None else jnp.where(lane == at, value, merged)
                sent[chunk * slabs + slab, field * 8 : field * 8 + 8, :] = merged
        return None

    def near_copy(field, slab, target):
        part = pl.ds(field * 8, 8)
        return pltpu.make_async_remote_copy(
            src_ref=sent.at[slab, part],
            dst_ref=near.at[pen if field else slot, part],
            send_sem=sem.at[1],
            recv_sem=sem.at[2 + 9 * field],
            device_id=(grp, target),
            device_id_type=MESH,
        )

    def far_copy(slab, target, piece):
        return pltpu.make_async_remote_copy(
            src_ref=sent.at[slab, pl.ds(0, 8)],
            dst_ref=far.at[slot],
            send_sem=sem.at[3],
            recv_sem=sem.at[4 + 8 * piece],
            device_id=(other, target),
            device_id_type=MESH,
        )

    def nth(at):
        place = (pen + at) % (2 * slabs)
        slab = nth_chunk(at // (2 * slabs)) * slabs + place % slabs
        return slab, jnp.where(place < slabs, slab, pens - 1 - slab)

    def send_near(field, low, high):
        def body(at, carry):
            slab, target = nth(at)

            @pl.when(target != pen)
            def _():
                near_copy(field, slab, target).start()

            return carry

        lax.fori_loop(low * 2 * slabs, high * 2 * slabs, body, 0, unroll=4 if high is chunks else 1)

    def send_far(low, high):
        def body(at, carry):
            far_copy(*nth(at), at // (4 * slabs)).start()
            return carry

        lax.fori_loop(low * 2 * slabs, high * 2 * slabs, body, 0, unroll=4 if high is chunks else 1)

    across = pen // 4 % 4 + pen % 4
    hold = jnp.where(half == 0, (pen // 16 + across) // 2, across * 2 // 3)
    hold = jnp.maximum(chunks - 1 - hold, 0)

    def chunk_step(step, carry):
        transform(step)

        @pl.when(step == hold)
        def _():
            pl.semaphore_wait(barrier, jnp.where(half == 0, pens, 2 * pens))

        low = jnp.where(step == hold, 0, step)

        @pl.when((half == 1) & (step == hold))
        def _():
            signal(ready, device_id=(other, pen))

        @pl.when((half == 1) & (step >= hold))
        def _():
            send_far(low, step + 1)

        @pl.when((half == 0) & (step >= hold))
        def _():
            send_near(0, low, step + 1)

        return carry

    lax.fori_loop(0, chunks, chunk_step, 0)
    keep_v = pltpu.make_async_copy(
        sent.at[own_slab, pl.ds(0, 8)], near.at[slot, pl.ds(0, 8)], sem.at[5]
    )
    keep_u = pltpu.make_async_copy(
        sent.at[own_slab, pl.ds(8, 8)], near.at[pen, pl.ds(8, 8)], sem.at[13]
    )
    keep_v.start()
    keep_u.start()

    @pl.when(half == 0)
    def _():
        pl.semaphore_wait(ready, 1)
        send_far(0, chunks)

    @pl.when(half == 1)
    def _():
        send_near(0, 0, chunks)

    send_near(1, 0, chunks)

    block = ky_ref[:, pl.ds(pl.multiple_of(own_slab // 4 * 128, 128), 128)]
    lane1 = lax.broadcasted_iota(jnp.int32, (1, 128), 1)
    waves = jnp.zeros((1, 128), jnp.int32)
    for at in range(4):
        shifted = pltpu.roll(block, (at - own_slab % 4 + 4) % 4 * PER_SLAB, 1)
        waves = jnp.where(lane1 // PER_SLAB == at, shifted, waves)
    alone = jnp.broadcast_to((waves == 0) | (waves == length_y // 2), (128, 128))
    row = lax.broadcasted_iota(jnp.int32, (128, 128), 0)
    column = lax.broadcasted_iota(jnp.int32, (128, 128), 1)
    plain = jnp.where((row == column) & ~(alone & (row < 64)), 1.0, 0.0)
    reverse = row // PER_SLAB * PER_SLAB + PER_SLAB - 1 - row % PER_SLAB
    turned = jnp.where((reverse == column) & ~alone, jnp.where(row < 64, 1.0, -1.0), 0.0)
    turned = jnp.where((reverse - 64 == column) & alone, -1.0, turned)
    pick = jnp.where(mirrored, turned, plain).astype(jnp.bfloat16)
    pick = jnp.concatenate([pick, pick, pick], 1)
    flip = jnp.where(mirrored, -1.0, 1.0)

    load.wait()
    keep_v.wait()
    keep_u.wait()
    ahead, behind = 1 + 2 * core, 3 - 2 * core

    def filtered(block, data, kept):
        high, low = split(data)
        taps = filters[block]
        size = data.shape[0]
        wide = jnp.dot(
            taps[:, :size],
            jnp.concatenate([high, low], 1),
            preferred_element_type=jnp.float32,
        )
        narrow = jnp.dot(taps[:, size:], high, preferred_element_type=jnp.float32)
        total = wide[:, :128] + wide[:, 128:] + narrow
        return total if kept is None else total + kept

    def received(at):
        count = near.at[pl.ds(0, pens - 1), pl.ds(0, 8)]
        pltpu.make_async_copy(count, count, sem.at[at]).wait()

    received(2)
    own_data = near[:, 0:8, :].reshape(depth, 128)
    side_out[...] = filtered(ahead, own_data, None)
    near_side[...] = filtered(0, own_data, None)
    def far_part(block, piece, rows):
        data, high_taps, low_taps = [], [], []
        for at in range(2):
            sender = (own_class + 2 * chunks - 2 * piece - at) % chunks
            cells = 2 * slabs * 8
            first = pl.multiple_of(sender * cells, cells)
            data.append(far[pl.ds(sender * 2 * slabs, 2 * slabs)].reshape(cells, 128))
            high_taps.append(filters[block, rows, pl.ds(first, cells)])
            low_taps.append(filters[block, rows, pl.ds(first + depth, cells)])
        high, low = split(jnp.concatenate(data, 0))
        wide = jnp.dot(
            jnp.concatenate(high_taps, 1),
            jnp.concatenate([high, low], 1),
            preferred_element_type=jnp.float32,
        )
        narrow = jnp.dot(
            jnp.concatenate(low_taps, 1), high, preferred_element_type=jnp.float32
        )
        return wide[:, :128] + wide[:, 128:] + narrow

    def far_received(piece):
        count = far.at[pl.ds(0, pens // 2)]
        pltpu.make_async_copy(count, count, sem.at[4 + 8 * piece]).wait()

    every = pl.ds(0, depth)
    far_received(0)
    side_out[...] += far_part(behind, 0, every)
    near_side[...] += far_part(2, 0, every)
    far_received(1)
    swaps = []
    for at in range(2):
        rows = pl.ds(at * depth // 2, depth // 2)
        side_out[rows, :] += far_part(behind, 1, rows)
        swaps.append(
            pltpu.make_async_remote_copy(
                src_ref=side_out.at[rows],
                dst_ref=side_in.at[rows],
                send_sem=sem.at[6 + 8 * at],
                recv_sem=sem.at[7 + 8 * at],
                device_id=(sibling, pen),
                device_id_type=MESH,
            )
        )
        swaps[at].start()
    far_side[...] = near_side[...] + far_part(2, 1, every)
    received(11)
    for swap in swaps:
        swap.wait()
    total = near[:, 8:16, :].reshape(depth, 128) + flip * (far_side[...] + side_in[...])
    high, low = split(total)
    lowest = (total - high.astype(jnp.float32) - low.astype(jnp.float32)).astype(jnp.bfloat16)
    out_ref[...] = lax.dot_general(
        pick,
        jnp.concatenate([high, low, lowest], 1),
        (((1,), (1,)), ((), ())),
        preferred_element_type=jnp.float32,
    )
    both = near.at[pl.ds(0, pens - 1)]
    pltpu.make_async_copy(both, both, sem.at[1]).wait()
    pltpu.make_async_copy(far, far, sem.at[3]).wait()


def filter_table(length, groups):
    waves = np.arange(length)
    scale = np.where(waves < length // 2, waves, waves - length).astype(np.float64)
    scale[length // 2] = 0.0
    taps = np.fft.ifft(2.0 / length * scale).imag
    depth = length // groups
    cell = np.arange(depth)
    pens = depth // 8
    lower = np.arange(pens // 2).reshape(-1, WAVES // PER_SLAB)
    pen = np.concatenate([lower, pens - 1 - lower], 1).reshape(-1, 1)
    source = (pen * 8 + np.arange(8)).reshape(-1)
    table = np.stack([taps[(depth * d + cell[:, None] - source[None, :]) % length] for d in range(groups)])
    table = table.astype(np.float32)
    high = table.astype(jnp.bfloat16)
    low = (table - high.astype(np.float32)).astype(jnp.bfloat16)
    return np.concatenate([high, low], 2)


def on_device(u_field, v_field, ky_order):
    planes, entry_rows, length_y = u_field.shape
    pens = lax.axis_size("pen")
    groups = lax.axis_size("grp")
    depth = entry_rows * pens
    table = jnp.asarray(filter_table(depth * groups, groups))
    inputs = (u_field, v_field, ky_order.reshape(1, length_y), table)
    inputs = [pltpu.with_memory_space_constraint(value, pltpu.HBM) for value in inputs]
    vmem = pl.BlockSpec(memory_space=pltpu.VMEM)
    result = pl.pallas_call(
        functools.partial(kernel, (length_y, pens, depth)),
        out_shape=jax.ShapeDtypeStruct((128, depth), jnp.float32),
        in_specs=[pl.BlockSpec(memory_space=pltpu.HBM)] * 4,
        out_specs=vmem,
        scratch_shapes=[
            pltpu.VMEM(u_field.shape, jnp.float32),
            pltpu.VMEM(v_field.shape, jnp.float32),
            pltpu.VMEM((1, length_y), jnp.int32),
            pltpu.VMEM((length_y // BLOCK * 32, 3 * BLOCK), jnp.bfloat16),
            pltpu.VMEM((pens // 2, 16, 128), jnp.float32),
            pltpu.VMEM((pens, 16, 128), jnp.float32),
            pltpu.VMEM((pens, 8, 128), jnp.float32),
            pltpu.VMEM((depth, 128), jnp.float32),
            pltpu.VMEM((depth, 128), jnp.float32),
            pltpu.VMEM((depth, 128), jnp.float32),
            pltpu.VMEM((depth, 128), jnp.float32),
            pltpu.VMEM((groups, depth, 2 * depth), jnp.bfloat16),
            pltpu.SemaphoreType.DMA((16,)),
            pltpu.SemaphoreType.REGULAR,
        ],
        compiler_params=pltpu.CompilerParams(
            collective_id=0, has_side_effects=True, vmem_limit_bytes=32 * 1024 * 1024
        ),
    )(*inputs)
    result = result.reshape(2, planes, length_y // pens, depth)
    return jnp.transpose(result, (3, 0, 1, 2))


def solution(mesh):
    placed = (P(None, ("grp", "pen"), None), P(None, ("grp", "pen"), None), P())
    return jax.shard_map(
        on_device,
        mesh=mesh,
        in_specs=placed,
        out_specs=P("grp", None, None, "pen"),
        check_vma=False,
    )
```
